32 devices in a mesh: sec: 2 (over core), elem: 16 (over z, y, x).
Axes of the slice: x: 2, y: 2, z: 4, core: 2. Of those that a mesh axis runs over, the one named last changes fastest.
Arguments:
- fields: float32 [2, 320, 16384], P('sec', None, 'elem'), may hold values from -6 to 6
- jacobian: float32 [2, 16384], P('sec', 'elem'), may hold values from 0.25 to 2.5
- face_links: int32 [2, 6, 16384], P('sec', None, 'elem'), may hold values from 0 to 1535, as said below
- volume_matrix: float32 [2, 320, 320], P('sec'), may hold values from -0.3125 to 0.3125
- face_matrices: float32 [2, 6, 320, 320], P('sec'), may hold values from -0.3125 to 0.3125
- patterns: float32 [4, 64, 64], replicated, may hold values from 0 to 0.03125
- donor_index: int32 [2, 2048], P('sec', 'elem'), may hold values from 0 to 1023
- pattern_index: int32 [2, 2048], P('sec', 'elem'), may hold values from 0 to 3
- receivers: int32 [2, 2048], P('sec', 'elem'), may hold values from -1 to 1023, as said below
Outputs:
- advanced: float32 [2, 320, 16384], P('sec', None, 'elem')
The draws below stay inside these ranges and needn't reach their ends.
Inputs may be any that keep to these rules, and one draw needn't show every extreme that they name: face_links[s, f, g] counts from the lowest rim element of the device holding element g; index 256 is that device's first own element. receivers holds on each device 8 slots for each device of the other section, source-major; -1 marks an empty slot, other entries on one device are distinct; in every draw some device gets 8 blocks from every device of the other section.
All inputs are finite; a program needn't handle non-finite values.
Results may differ from the reference program's by a relative error of at most 0.0001.
Values sent between devices are 32-bit elements; how exact they have to be, the bound alone decides.
A program may use at most 64 MiB of HBM per device.

```python
import math
import jax
import jax.numpy as jnp
from jax import lax

VARS = 5
NODES = 64
E_DEV = 1024
HALO = 256
CAP = 8
NPAT = 4
COMPONENTS = 320
NE = 16384
SLOTS = 128
TOTAL_SLOTS = 2048
N_ELEM = 16


def draw_face_links(key, part):
    subkeys = jax.random.split(jax.random.fold_in(key, 7), 3)
    grid_shape = (2, 6, NE)
    position = jnp.arange(NE, dtype=jnp.int32) % E_DEV
    near_reach = min(16, HALO)
    short_reach = jax.random.randint(subkeys[0], grid_shape, 1, near_reach + 1, dtype=jnp.int32)
    medium = jax.random.randint(subkeys[1], grid_shape, 1, HALO // 2 + 1, dtype=jnp.int32)
    far_reach = jax.random.randint(subkeys[2], grid_shape, HALO // 2, HALO + 1, dtype=jnp.int32)
    distance = jnp.concatenate([short_reach[:, 0:2], medium[:, 2:4], far_reach[:, 4:6]], axis=1)
    direction = jnp.array([-1, 1, -1, 1, -1, 1], jnp.int32)[None, :, None]
    neighbours = position[None, None, :] + HALO + direction * distance
    face_ids = jnp.arange(6, dtype=jnp.int32)[None, :, None]
    neighbours = jnp.where((face_ids == 4) & (position == 0)[None, None, :], 0, neighbours)
    neighbours = jnp.where((face_ids == 5) & (position == E_DEV - 1)[None, None, :], E_DEV + 2 * HALO - 1, neighbours)
    return neighbours.astype(jnp.int32)


def draw_receivers(key, part):
    sections = []
    for section in range(2):
        subkeys = jax.random.split(jax.random.fold_in(key, 11 + section), 3)
        counts = jax.random.randint(subkeys[0], (N_ELEM, N_ELEM), CAP // 2, CAP + 1, dtype=jnp.int32)
        source = jnp.arange(N_ELEM, dtype=jnp.int32)[:, None]
        target = jnp.arange(N_ELEM, dtype=jnp.int32)[None, :]
        quarter = N_ELEM // 4
        reach = 3 * N_ELEM // 4
        if section == 1:
            banded = (target - source // quarter * quarter) % N_ELEM < reach
        else:
            banded = (source - target // quarter * quarter) % N_ELEM < reach
        busiest = jax.random.randint(subkeys[1], (), 0, N_ELEM, dtype=jnp.int32)
        counts = jnp.where(target == busiest, CAP, jnp.where(banded, counts, 0))
        orders = jax.vmap(lambda subkey: jax.random.permutation(subkey, E_DEV))(jax.random.split(subkeys[2], N_ELEM)).astype(jnp.int32)
        leading = orders[:, :1]
        orders = jnp.where(orders == E_DEV - 1, leading, orders)
        orders = orders.at[:, 0].set(E_DEV - 1)
        slot_number = jnp.arange(N_ELEM * CAP, dtype=jnp.int32)
        sender = slot_number // CAP
        within = slot_number % CAP
        limit = jnp.transpose(counts)[:, sender]
        values = jnp.where(within[None, :] < limit, orders[:, :N_ELEM * CAP], -1)
        sections.append(values.reshape(-1))
    return jnp.stack(sections).astype(jnp.int32)


def set_ends(values, key, smallest, top_value):
    shape = values.shape
    spot = [jax.random.randint(jax.random.fold_in(key, axis), (), 0, shape[axis]) for axis in range(len(shape))]
    values = values.at[tuple(spot)].set(smallest)
    longest = shape.index(max(shape))
    spot[longest] = (spot[longest] + 1) % shape[longest]
    return values.at[tuple(spot)].set(top_value)


def levels(key, extent, pieces, smallest, top_value):
    def one(dim, blocks):
        draws = jax.random.uniform(jax.random.fold_in(jax.random.fold_in(key, 6), dim), (blocks,), jnp.float32, smallest / len(pieces), top_value / len(pieces))
        return jnp.repeat(jnp.exp(draws), extent[dim] // blocks).reshape((-1,) + (1,) * (len(extent) - dim - 1))

    gain = one(*pieces[0])
    for cut in pieces[1:]:
        gain = gain * one(*cut)
    return gain


def noise(key, dims, spread, bound, cuts=(), kind=jnp.bfloat16):
    drawn = jax.random.normal(key, dims, jnp.float32) * spread
    if len(cuts) > 0:
        drawn = levels(key, dims, cuts, -0.22, 0.18) * drawn
    return jnp.clip(drawn, min=-bound, max=bound).astype(kind)


def setup_inputs(seed: int = 0) -> dict:
    seeds = jax.random.split(jax.random.key(seed), 10)
    return {
        "fields": noise(seeds[0], (2, COMPONENTS, NE), 1.0, 6.0, ((0, 2), (2, 16)), jnp.float32),
        "jacobian": jnp.clip(jnp.exp(math.log(2.5) - 2.3025851 * jax.random.uniform(seeds[1], (2, NE), jnp.float32) ** levels(seeds[1], (2, NE), ((0, 2), (1, 16)), -0.2, 0.2)), 0.25, 2.5),
        "face_links": draw_face_links(jax.random.fold_in(seeds[9], 71), 0),
        "volume_matrix": noise(seeds[3], (2, COMPONENTS, COMPONENTS), COMPONENTS ** -0.5, 0.3125, ((0, 2),), jnp.float32),
        "face_matrices": noise(seeds[4], (2, 6, COMPONENTS, COMPONENTS), COMPONENTS ** -0.5, 0.3125, ((0, 2),), jnp.float32),
        "patterns": jnp.clip(jax.random.uniform(seeds[5], (NPAT, NODES, NODES), jnp.float32, 0.0, 0.03125), 0.0, 0.03125),
        "donor_index": set_ends(jax.random.randint(seeds[6], (2, TOTAL_SLOTS), 0, E_DEV), jax.random.fold_in(seeds[6], 1), 0, E_DEV - 1).astype(jnp.int32),
        "pattern_index": set_ends(jax.random.randint(seeds[7], (2, TOTAL_SLOTS), 0, NPAT), jax.random.fold_in(seeds[7], 1), 0, NPAT - 1).astype(jnp.int32),
        "receivers": draw_receivers(jax.random.fold_in(seeds[9], 71), 0),
    }


time_step = 0.25


def section_rate(values, inverse_volume, neighbours, volume_block, face_blocks):
    padded = jnp.pad(values, ((0, 0), (HALO, HALO)))
    element = jnp.arange(NE, dtype=jnp.int32)
    anchor = (element // E_DEV) * E_DEV
    summed = jnp.dot(volume_block, values, precision=lax.Precision.HIGHEST, preferred_element_type=jnp.float32)
    for direction in range(6):
        column = (anchor + neighbours[direction]).astype(jnp.int32)
        summed = summed + jnp.dot(face_blocks[direction], jnp.take(padded, column, axis=1), precision=lax.Precision.HIGHEST, preferred_element_type=jnp.float32)
    return inverse_volume[None, :] * summed


def interpolate(values, donors, choose, patterns):
    columns = jnp.take(values, donors, axis=1).reshape(VARS, NODES, -1)
    result = jnp.zeros_like(columns)
    for which_one in range(NPAT):
        mapped = jnp.einsum("mn,vnc->vmc", patterns[which_one], columns, precision=lax.Precision.HIGHEST)
        result = jnp.where(choose[None, None, :] == which_one, mapped, result)
    return result.reshape(VARS * NODES, -1)


def fringe(fields, donor_index, pattern_index, receivers, patterns):
    slot_owner = jnp.arange(TOTAL_SLOTS, dtype=jnp.int32) // SLOTS
    blocks = []
    for section in range(2):
        donors = (slot_owner * E_DEV + donor_index[section]).astype(jnp.int32)
        blocks.append(interpolate(fields[section], donors, pattern_index[section], patterns))
    updated = []
    for section in range(2):
        source = blocks[1 - section].reshape(VARS * NODES, N_ELEM, N_ELEM, CAP)
        source = jnp.transpose(source, (0, 2, 1, 3)).reshape(VARS * NODES, TOTAL_SLOTS)
        target = receivers[section]
        place = jnp.where(target >= 0, slot_owner * E_DEV + target, NE).astype(jnp.int32)
        updated.append(fields[section].at[:, place].set(source, mode="drop"))
    return jnp.stack(updated)


def rate(values, jacobian, face_links, volume_matrix, face_matrices):
    return jnp.stack([section_rate(values[section], jacobian[section], face_links[section], volume_matrix[section], face_matrices[section]) for section in range(2)])


def reference(fields, jacobian, face_links, volume_matrix, face_matrices, patterns, donor_index, pattern_index, receivers):
    first_segment = fringe(fields, donor_index, pattern_index, receivers, patterns)
    middle = first_segment + time_step * rate(first_segment, jacobian, face_links, volume_matrix, face_matrices)
    second = fringe(middle, donor_index, pattern_index, receivers, patterns)
    return 0.5 * first_segment + 0.5 * (second + time_step * rate(second, jacobian, face_links, volume_matrix, face_matrices))
```

```python
import functools

import jax
import jax.numpy as jnp
from jax import lax
from jax.experimental import pallas as pl
from jax.experimental.pallas import tpu as pltpu
from jax.sharding import PartitionSpec as P

HALO = 256
LANES = 128
CHUNK = 256
ROWS = 5
FACES = 6
STEP = 0.25
MESH = pl.DeviceIdType.MESH
F32 = jnp.float32
BF16 = jnp.bfloat16


def split(value):
    high = value.astype(BF16)
    return high, (value - high.astype(F32)).astype(BF16)


def cross(a, b):
    return lax.dot_general(a, b, (((1,), (1,)), ((), ())), preferred_element_type=F32)


def iota(shape, dim):
    return lax.broadcasted_iota(jnp.int32, shape, dim)


def column(row):
    return jnp.transpose(jnp.broadcast_to(row.astype(F32), (LANES, LANES))).astype(jnp.int32)


def kernel(
    n,
    index,
    fields,
    jacobian,
    links,
    donors,
    choose,
    receivers,
    patterns,
    volume_hbm,
    faces_hbm,
    out,
    volume,
    faces,
    first,
    state,
    total,
    halves,
    give,
    twice,
    mixed,
    donated,
    outgoing,
    landed,
    take,
    hit,
    table,
    gathered,
    even,
    odd,
    weights,
    rims,
    rim_operand,
    made_high,
    made_low,
    onehot,
    block_send,
    block_recv,
    rim_send,
    rim_recv,
    load,
):
    sec, me = lax.axis_index("sec"), lax.axis_index("elem")
    other = 1 - sec
    components, elements = fields.shape
    slots = donors.shape[1]
    per_device = slots // n
    rows = 2 * per_device + per_device // 2
    tail = components - 2 * LANES
    width = 8 * LANES
    half = HALO // 2

    barrier = pltpu.get_barrier_semaphore()
    for j in range(n):
        pl.semaphore_signal(barrier, inc=1, device_id=(other, j), device_id_type=MESH)

    @pl.when(me > 0)
    def _():
        pl.semaphore_signal(barrier, inc=1, device_id=(sec, me - 1), device_id_type=MESH)

    @pl.when(me < n - 1)
    def _():
        pl.semaphore_signal(barrier, inc=1, device_id=(sec, me + 1), device_id_type=MESH)

    volume_copy = pltpu.make_async_copy(volume_hbm, volume, load.at[0])
    faces_copy = pltpu.make_async_copy(faces_hbm, faces, load.at[1])
    volume_copy.start()
    faces_copy.start()

    for b in range(slots // LANES):
        rows_b = slice(b * LANES, (b + 1) * LANES)
        donor = column(donors[:, rows_b])
        for t in range(elements // LANES):
            lane = iota((LANES, LANES), 1) + t * LANES
            one = jnp.where(donor == lane, 1.0, 0.0).astype(BF16)
            give[rows_b, t * LANES : (t + 1) * LANES] = one
            give[rows_b, elements + t * LANES : elements + (t + 1) * LANES] = one
    kinds = [column(choose[:, b * LANES : (b + 1) * LANES]) for b in range(slots // LANES)]
    count = patterns.shape[0]
    for p in range(count):
        one = patterns[p]
        none = jnp.zeros_like(one)
        both = jnp.concatenate(
            [jnp.concatenate([one, none], axis=1), jnp.concatenate([none, one], axis=1)], axis=0
        )
        high, low = split(both)
        for part, value in enumerate((high, high, low)):
            at = (part * count + p) * LANES
            twice[:, at : at + LANES] = value

    def prepare_receivers():
        for t in range(elements // LANES):
            lane = iota((LANES, LANES), 1) + t * LANES
            here = slice(t * LANES, (t + 1) * LANES)
            seen = jnp.zeros((1, LANES), F32)
            for b in range(slots // LANES):
                one = jnp.where(column(receivers[:, b * LANES : (b + 1) * LANES]) == lane, 1.0, 0.0)
                seen = seen + jnp.sum(one, axis=0, keepdims=True)
                take[b * LANES : (b + 1) * LANES, here] = one.astype(BF16)
                take[slots + b * LANES : slots + (b + 1) * LANES, here] = one.astype(BF16)
            hit[:, here] = seen

    def prepare_weights():
        volume_copy.wait()
        faces_copy.wait()
        for f in range(FACES + 1):
            matrix = volume if f == FACES else faces.at[f]
            high, low = split(matrix[:, 0 : 2 * LANES])
            ends = matrix[:, 2 * LANES : components]
            end_high, end_low = split(jnp.concatenate([ends, ends], axis=1))
            lane = iota(end_low.shape, 1)
            end_low = jnp.where(lane < tail, end_low.astype(F32), 0.0).astype(BF16)
            at = f * width
            weights[:, at : at + 2 * LANES] = high
            weights[:, at + 2 * LANES : at + 4 * LANES] = high
            weights[:, at + 4 * LANES : at + 6 * LANES] = low
            weights[:, at + 6 * LANES : at + 7 * LANES] = end_high
            weights[:, at + 7 * LANES : at + 8 * LANES] = end_low

    def prepare_onehot():
        def body(f, carry):
            for h in range(2):
                for side in range(2):
                    begin = side * (HALO + elements) + h * half
                    for t in range(elements // CHUNK):
                        here = slice(t * CHUNK, (t + 1) * CHUNK)
                        row = links[pl.ds(f, 1), here]
                        one = jnp.where(row == iota((half, CHUNK), 0) + begin, 1.0, 0.0)
                        at = pl.multiple_of((h * FACES + f) * HALO + side * half, half)
                        onehot[pl.ds(at, half), here] = one.astype(BF16)
            return carry

        lax.fori_loop(0, FACES, body, 0)

    def rim_copy(stage, source, side, h):
        target = me - 1 if side == 0 else me + 1
        begin = h * half if side == 0 else elements - HALO + h * half
        return pltpu.make_async_remote_copy(
            src_ref=source.at[:, pl.ds(begin, half)],
            dst_ref=rims.at[stage, h, :, pl.ds((1 - side) * half, half)],
            send_sem=rim_send.at[stage, side, h],
            recv_sem=rim_recv.at[stage, 1 - side, h],
            device_id=(sec, target),
            device_id_type=MESH,
        )

    for stage in range(2):
        source = fields if stage == 0 else out
        patched = first if stage == 0 else state

        high, low = split(source[...])
        halves[:, 0:elements] = high
        halves[:, elements:] = low
        donated[:, 0:components] = cross(give[...], halves[...])
        for b in range(slots // LANES):
            for k in range(3):
                piece = donated[b * LANES : (b + 1) * LANES, k * LANES : (k + 1) * LANES]
                if k == 2:
                    piece = jnp.where(iota(piece.shape, 1) < tail, piece, 0.0)
                high = piece.astype(BF16).astype(F32)
                for p in range(count):
                    mask = kinds[b] == p
                    big = jnp.where(mask, high, 0.0).astype(BF16)
                    small = jnp.where(mask, piece - high, 0.0).astype(BF16)
                    row = k * slots + b * LANES
                    for part, value in enumerate((big, small, big)):
                        at = (part * count + p) * LANES
                        mixed[row : row + LANES, at : at + LANES] = value
        result = cross(mixed[...], twice[...])
        quarter = per_device // 2
        for j in range(n):
            at, slot = j * rows, j * per_device
            outgoing[at : at + per_device, :] = result[slot : slot + per_device]
            outgoing[at + per_device : at + 2 * per_device, :] = result[slots + slot : slots + slot + per_device]
            ends = result[2 * slots + slot : 2 * slots + slot + per_device]
            outgoing[at + 2 * per_device : at + rows, :] = ends[:quarter] + pltpu.roll(ends, tail, 1)[quarter:]

        if stage == 0:
            heard = n + (me > 0).astype(jnp.int32) + (me < n - 1).astype(jnp.int32)
            pl.semaphore_wait(barrier, heard)

        def block_copy(j):
            return pltpu.make_async_remote_copy(
                src_ref=outgoing.at[pl.ds(j * rows, rows)],
                dst_ref=landed.at[stage, pl.ds(me * rows, rows)],
                send_sem=block_send.at[stage, j],
                recv_sem=block_recv.at[stage, me],
                device_id=(other, j),
                device_id_type=MESH,
            )

        def arrived(j):
            return pltpu.make_async_remote_copy(
                src_ref=outgoing.at[pl.ds(j * rows, rows)],
                dst_ref=landed.at[stage, pl.ds(j * rows, rows)],
                send_sem=block_send.at[stage, j],
                recv_sem=block_recv.at[stage, j],
                device_id=(other, j),
                device_id_type=MESH,
            )

        for j in range(n):
            block_copy(j).start()
        if stage == 0:
            prepare_receivers()
            prepare_weights()
        for j in range(n):
            arrived(j).wait_recv()

        for b in range(slots // LANES):
            pieces = [[], [], []]
            for j in range(b * LANES // per_device, (b + 1) * LANES // per_device):
                at = j * rows
                pieces[0].append(landed[stage, at : at + per_device, :])
                pieces[1].append(landed[stage, at + per_device : at + 2 * per_device, :])
                ends = landed[stage, at + 2 * per_device : at + rows, :]
                pieces[2].append(jnp.concatenate([ends, pltpu.roll(ends, tail, 1)], axis=0))
            for k in range(3):
                count_k = LANES if k < 2 else tail
                high, low = split(jnp.transpose(jnp.concatenate(pieces[k], axis=0))[:count_k])
                here = slice(k * LANES, k * LANES + count_k)
                mixed_rows = halves
                mixed_rows[here, b * LANES : (b + 1) * LANES] = high
                mixed_rows[here, slots + b * LANES : slots + (b + 1) * LANES] = low
        chunks = elements // CHUNK
        for c in [0, chunks - 1] + list(range(1, chunks - 1)):
            here = slice(c * CHUNK, (c + 1) * CHUNK)
            moved = jnp.dot(halves[:, 0 : 2 * slots], take[:, here], preferred_element_type=F32)
            patched[:, here] = jnp.where(hit[:, here] > 0.5, moved, source[:, here])
            for side in range(2):
                if c == (0 if side == 0 else chunks - 1):

                    @pl.when(me > 0 if side == 0 else me < n - 1)
                    def _():
                        for h in range(2):
                            rim_copy(stage, patched, side, h).start()

        for t in range(elements // LANES):
            here = slice(t * LANES, (t + 1) * LANES)
            at = t * LANES * ROWS
            for k in range(2):
                piece = jnp.transpose(patched[k * LANES : (k + 1) * LANES, here])
                high = piece.astype(BF16).astype(F32)
                table[pl.ds(at + k, LANES, stride=ROWS), :] = high
                table[pl.ds(at + 2 + k, LANES, stride=ROWS), :] = piece - high
            ends = patched[2 * LANES : components, here]
            high = ends.astype(BF16).astype(F32)
            table[pl.ds(at + 4, LANES, stride=ROWS), :] = jnp.transpose(
                jnp.concatenate([high, ends - high], axis=0)
            )
        table[elements * ROWS :, :] = jnp.zeros((8, LANES), F32)
        if stage == 0:
            prepare_onehot()

        def to_operand(source_ref, target, f):
            for k in range(ROWS):
                target[f * ROWS + k] = source_ref[pl.ds(k, CHUNK, stride=ROWS), :].astype(BF16)

        def gather(c, target):
            for f in range(FACES):
                where = gathered.at[f]
                for e in range(CHUNK):
                    row = index[f * elements + c * CHUNK + e]
                    where[e * ROWS : (e + 1) * ROWS, :] = table[pl.ds(row, ROWS), :]
                to_operand(where, target, f)
            size = CHUNK * ROWS
            to_operand(table.at[pl.ds(c * size, size)], target, FACES)

        def contract(c, target):
            parts = []
            for f in range(FACES + 1):
                parts += [target[f * ROWS + k] for k in (0, 1, 2, 3, 0, 1, 4, 4)]
            total[c] = cross(weights[...], jnp.concatenate(parts, axis=1))

        gather(0, even)

        def own(i, carry):
            gather(2 * i + 1, odd)
            contract(2 * i, even)
            gather(lax.rem(2 * i + 2, chunks), even)
            contract(2 * i + 1, odd)
            return carry

        lax.fori_loop(0, chunks // 2, own, 0)

        for h in range(2):
            for side in range(2):
                inside = me > 0 if side == 0 else me < n - 1
                where = rims.at[stage, h, :, pl.ds(side * half, half)]

                @pl.when(inside)
                def _():
                    rim_copy(stage, patched, 1 - side, h).wait_recv()

                @pl.when(jnp.logical_not(inside))
                def _():
                    where[...] = jnp.zeros((components, half), F32)

            high, low = split(rims[stage, h])
            top = 2 * LANES
            rim_operand[0:top, :] = high[:top]
            rim_operand[top : 2 * top, :] = low[:top]
            rim_operand[2 * top : 3 * top, :] = high[:top]
            at = 3 * top
            for m, value in enumerate((high[top:], low[top:], high[top:], jnp.zeros_like(high[top:]))):
                rim_operand[at + m * tail : at + (m + 1) * tail, :] = value
            for f in range(FACES):
                made = jnp.dot(
                    weights[:, f * width : (f + 1) * width], rim_operand[...], preferred_element_type=F32
                )
                high, low = split(made)
                made_high[:, f * HALO : (f + 1) * HALO] = high
                made_low[:, f * HALO : (f + 1) * HALO] = low

            for c in range(chunks):
                here = slice(c * CHUNK, (c + 1) * CHUNK)
                chosen = onehot[h * FACES * HALO : (h + 1) * FACES * HALO, here]
                sum_c = total[c]
                sum_c = sum_c + jnp.dot(made_high[...], chosen, preferred_element_type=F32)
                sum_c = sum_c + jnp.dot(made_low[...], chosen, preferred_element_type=F32)
                if h == 0:
                    total[c] = sum_c
                else:
                    stepped = patched[:, here] + (STEP * jacobian[:, here]) * sum_c
                    if stage == 0:
                        out[:, here] = stepped
                    else:
                        out[:, here] = 0.5 * first[:, here] + 0.5 * stepped

        for j in range(n):
            block_copy(j).wait_send()
        for side in range(2):

            @pl.when(me > 0 if side == 0 else me < n - 1)
            def _():
                for h in range(2):
                    rim_copy(stage, patched, side, h).wait_send()


def local(
    n,
    fields,
    jacobian,
    face_links,
    volume_matrix,
    face_matrices,
    patterns,
    donor_index,
    pattern_index,
    receivers,
):
    components, elements = fields.shape[1:]
    slots = donor_index.shape[1]
    rows = slots // n * 5 // 2
    inner = face_links[0] - HALO
    index = jnp.where((inner >= 0) & (inner < elements), inner, elements) * ROWS
    smem = pl.BlockSpec(memory_space=pltpu.SMEM)
    vmem = pl.BlockSpec(memory_space=pltpu.VMEM)
    hbm = pl.BlockSpec(memory_space=pl.ANY)
    chunks = elements // CHUNK
    width = 8 * LANES
    count = patterns.shape[0]
    result = pl.pallas_call(
        functools.partial(kernel, n),
        out_shape=jax.ShapeDtypeStruct((components, elements), F32),
        in_specs=[smem] + [vmem] * 7 + [hbm] * 2,
        out_specs=vmem,
        scratch_shapes=[
            pltpu.VMEM((components, components), F32),
            pltpu.VMEM((FACES, components, components), F32),
            pltpu.VMEM((components, elements), F32),
            pltpu.VMEM((components, elements), F32),
            pltpu.VMEM((chunks, components, CHUNK), F32),
            pltpu.VMEM((components, 2 * elements), BF16),
            pltpu.VMEM((slots, 2 * elements), BF16),
            pltpu.VMEM((LANES, 3 * count * LANES), BF16),
            pltpu.VMEM((3 * slots, 3 * count * LANES), BF16),
            pltpu.VMEM((slots, 3 * LANES), F32),
            pltpu.VMEM((n * rows, LANES), F32),
            pltpu.VMEM((2, n * rows, LANES), F32),
            pltpu.VMEM((2 * slots, elements), BF16),
            pltpu.VMEM((1, elements), F32),
            pltpu.VMEM((elements * ROWS + 8, LANES), F32),
            pltpu.VMEM((FACES, CHUNK * ROWS, LANES), F32),
            pltpu.VMEM(((FACES + 1) * ROWS, CHUNK, LANES), BF16),
            pltpu.VMEM(((FACES + 1) * ROWS, CHUNK, LANES), BF16),
            pltpu.VMEM((components, (FACES + 1) * width), BF16),
            pltpu.VMEM((2, 2, components, HALO), F32),
            pltpu.VMEM((width, HALO), BF16),
            pltpu.VMEM((components, FACES * HALO), BF16),
            pltpu.VMEM((components, FACES * HALO), BF16),
            pltpu.VMEM((2 * FACES * HALO, elements), BF16),
            pltpu.SemaphoreType.DMA((2, n)),
            pltpu.SemaphoreType.DMA((2, n)),
            pltpu.SemaphoreType.DMA((2, 2, 2)),
            pltpu.SemaphoreType.DMA((2, 2, 2)),
            pltpu.SemaphoreType.DMA((2,)),
        ],
        compiler_params=pltpu.CompilerParams(
            collective_id=0, has_side_effects=True, vmem_limit_bytes=62 * 1024 * 1024
        ),
    )(
        index.reshape(-1),
        fields[0],
        jacobian,
        face_links[0],
        donor_index,
        pattern_index,
        receivers,
        patterns,
        volume_matrix[0],
        face_matrices[0],
    )
    return result[None]


def solution(mesh):
    return jax.shard_map(
        functools.partial(local, mesh.shape["elem"]),
        mesh=mesh,
        in_specs=(
            P("sec", None, "elem"),
            P("sec", "elem"),
            P("sec", None, "elem"),
            P("sec", None, None),
            P("sec", None, None, None),
            P(),
            P("sec", "elem"),
            P("sec", "elem"),
            P("sec", "elem"),
        ),
        out_specs=P("sec", None, "elem"),
        check_vma=False,
    )
```

```python
import functools

import jax
import jax.numpy as jnp
from jax import lax
from jax.experimental import pallas as pl
from jax.experimental.pallas import tpu as pltpu
from jax.sharding import PartitionSpec as P

HALO = 256
LANES = 128
CHUNK = 256
ROWS = 5
FACES = 6
STEP = 0.25
MESH = pl.DeviceIdType.MESH
F32 = jnp.float32
BF16 = jnp.bfloat16


def split(value):
    high = value.astype(BF16)
    return high, (value - high.astype(F32)).astype(BF16)


def cross(a, b):
    return lax.dot_general(a, b, (((1,), (1,)), ((), ())), preferred_element_type=F32)


def iota(shape, dim):
    return lax.broadcasted_iota(jnp.int32, shape, dim)


def column(row):
    return jnp.transpose(jnp.broadcast_to(row.astype(F32), (LANES, LANES))).astype(jnp.int32)


def kernel(
    n,
    fields_hbm,
    jacobian_hbm,
    links_hbm,
    donors_hbm,
    choose_hbm,
    receivers_hbm,
    patterns_hbm,
    volume_hbm,
    faces_hbm,
    out_hbm,
    jacobian,
    links,
    donors,
    choose,
    receivers,
    patterns,
    reach,
    index,
    current,
    volume,
    faces,
    states,
    total,
    halves,
    give,
    twice,
    mixed,
    donated,
    outgoing,
    landed,
    take,
    hit,
    table,
    gathered,
    even,
    odd,
    weights,
    rims,
    rim_operand,
    made_high,
    made_low,
    onehot,
    block_send,
    block_recv,
    rim_send,
    rim_recv,
    load,
    store,
):
    sec, me = lax.axis_index("sec"), lax.axis_index("elem")
    other = 1 - sec
    components, elements = current.shape
    slots = donors.shape[1]
    per_device = slots // n
    rows = 2 * per_device + per_device // 2
    tail = components - 2 * LANES
    width = 8 * LANES
    half = HALO // 2

    barrier = pltpu.get_barrier_semaphore()
    for j in range(n):
        pl.semaphore_signal(barrier, inc=1, device_id=(other, j), device_id_type=MESH)

    @pl.when(me > 0)
    def _():
        pl.semaphore_signal(barrier, inc=1, device_id=(sec, me - 1), device_id_type=MESH)

    @pl.when(me < n - 1)
    def _():
        pl.semaphore_signal(barrier, inc=1, device_id=(sec, me + 1), device_id_type=MESH)

    pairs = (
        (donors_hbm, donors),
        (choose_hbm, choose),
        (patterns_hbm, patterns),
        (fields_hbm, current),
        (receivers_hbm, receivers),
        (links_hbm, links),
        (jacobian_hbm, jacobian),
        (volume_hbm, volume),
        (faces_hbm, faces),
    )
    loads = [pltpu.make_async_copy(src, dst, load.at[i]) for i, (src, dst) in enumerate(pairs)]
    for copy in loads:
        copy.start()
    index_copy = pltpu.make_async_copy(reach, index, load.at[len(loads)])

    for copy in loads[:3]:
        copy.wait()

    for b in range(slots // LANES):
        rows_b = slice(b * LANES, (b + 1) * LANES)
        donor = column(donors[:, rows_b])
        for t in range(elements // LANES):
            lane = iota((LANES, LANES), 1) + t * LANES
            one = jnp.where(donor == lane, 1.0, 0.0).astype(BF16)
            give[rows_b, t * LANES : (t + 1) * LANES] = one
            give[rows_b, elements + t * LANES : elements + (t + 1) * LANES] = one
    kinds = [column(choose[:, b * LANES : (b + 1) * LANES]) for b in range(slots // LANES)]
    count = patterns.shape[0]
    for p in range(count):
        one = patterns[p]
        none = jnp.zeros_like(one)
        both = jnp.concatenate(
            [jnp.concatenate([one, none], axis=1), jnp.concatenate([none, one], axis=1)], axis=0
        )
        high, low = split(both)
        for part, value in enumerate((high, high, low)):
            at = (part * count + p) * LANES
            twice[:, at : at + LANES] = value

    def prepare_index():
        for f in range(FACES):
            inner = links[f] - HALO
            owned = (inner >= 0) & (inner < elements)
            row = jnp.where(owned, inner, elements) * ROWS
            for t in range(elements // LANES):
                at = f * (elements // LANES) + t
                reach[at : at + 1, :] = row[:, t * LANES : (t + 1) * LANES]
        index_copy.start()

    def prepare_receivers():
        for t in range(elements // LANES):
            lane = iota((LANES, LANES), 1) + t * LANES
            here = slice(t * LANES, (t + 1) * LANES)
            seen = jnp.zeros((1, LANES), F32)
            for b in range(slots // LANES):
                one = jnp.where(column(receivers[:, b * LANES : (b + 1) * LANES]) == lane, 1.0, 0.0)
                seen = seen + jnp.sum(one, axis=0, keepdims=True)
                take[b * LANES : (b + 1) * LANES, here] = one.astype(BF16)
                take[slots + b * LANES : slots + (b + 1) * LANES, here] = one.astype(BF16)
            hit[:, here] = seen

    def prepare_weights():
        for f in range(FACES + 1):
            matrix = volume if f == FACES else faces.at[f]
            high, low = split(matrix[:, 0 : 2 * LANES])
            ends = matrix[:, 2 * LANES : components]
            end_high, end_low = split(jnp.concatenate([ends, ends], axis=1))
            lane = iota(end_low.shape, 1)
            end_low = jnp.where(lane < tail, end_low.astype(F32), 0.0).astype(BF16)
            at = f * width
            weights[:, at : at + 2 * LANES] = high
            weights[:, at + 2 * LANES : at + 4 * LANES] = high
            weights[:, at + 4 * LANES : at + 6 * LANES] = low
            weights[:, at + 6 * LANES : at + 7 * LANES] = end_high
            weights[:, at + 7 * LANES : at + 8 * LANES] = end_low

    def prepare_onehot():
        def body(f, carry):
            for h in range(2):
                for side in range(2):
                    begin = side * (HALO + elements) + h * half
                    for t in range(elements // CHUNK):
                        here = slice(t * CHUNK, (t + 1) * CHUNK)
                        row = links[f, :, here]
                        one = jnp.where(row == iota((half, CHUNK), 0) + begin, 1.0, 0.0)
                        at = pl.multiple_of((h * FACES + f) * HALO + side * half, half)
                        onehot[pl.ds(at, half), here] = one.astype(BF16)
            return carry

        lax.fori_loop(0, FACES, body, 0)

    def rim_copy(stage, source, side, h):
        target = me - 1 if side == 0 else me + 1
        begin = h * half if side == 0 else elements - HALO + h * half
        return pltpu.make_async_remote_copy(
            src_ref=source.at[:, pl.ds(begin, half)],
            dst_ref=rims.at[stage, h, :, pl.ds((1 - side) * half, half)],
            send_sem=rim_send.at[stage, side, h],
            recv_sem=rim_recv.at[stage, 1 - side, h],
            device_id=(sec, target),
            device_id_type=MESH,
        )

    def result_copy(c):
        here = pl.ds(c * CHUNK, CHUNK)
        return pltpu.make_async_copy(current.at[:, here], out_hbm.at[:, here], store.at[c])

    loads[3].wait()
    first = states.at[0]

    def segment(stage, carry):
        source = current
        patched = states.at[stage]
        begins = stage == 0

        high, low = split(source[...])
        halves[:, 0:elements] = high
        halves[:, elements:] = low
        donated[:, 0:components] = cross(give[...], halves[...])
        for b in range(slots // LANES):
            for k in range(3):
                piece = donated[b * LANES : (b + 1) * LANES, k * LANES : (k + 1) * LANES]
                if k == 2:
                    piece = jnp.where(iota(piece.shape, 1) < tail, piece, 0.0)
                high = piece.astype(BF16).astype(F32)
                for p in range(count):
                    mask = kinds[b] == p
                    big = jnp.where(mask, high, 0.0).astype(BF16)
                    small = jnp.where(mask, piece - high, 0.0).astype(BF16)
                    row = k * slots + b * LANES
                    for part, value in enumerate((big, small, big)):
                        at = (part * count + p) * LANES
                        mixed[row : row + LANES, at : at + LANES] = value
        result = cross(mixed[...], twice[...])
        quarter = per_device // 2
        for j in range(n):
            at, slot = j * rows, j * per_device
            outgoing[at : at + per_device, :] = result[slot : slot + per_device]
            outgoing[at + per_device : at + 2 * per_device, :] = result[slots + slot : slots + slot + per_device]
            ends = result[2 * slots + slot : 2 * slots + slot + per_device]
            outgoing[at + 2 * per_device : at + rows, :] = ends[:quarter] + pltpu.roll(ends, tail, 1)[quarter:]

        @pl.when(begins)
        def _():
            heard = n + (me > 0).astype(jnp.int32) + (me < n - 1).astype(jnp.int32)
            pl.semaphore_wait(barrier, heard)

        def block_copy(j):
            return pltpu.make_async_remote_copy(
                src_ref=outgoing.at[pl.ds(j * rows, rows)],
                dst_ref=landed.at[stage, pl.ds(me * rows, rows)],
                send_sem=block_send.at[stage, j],
                recv_sem=block_recv.at[stage, me],
                device_id=(other, j),
                device_id_type=MESH,
            )

        def arrived(j):
            return pltpu.make_async_remote_copy(
                src_ref=outgoing.at[pl.ds(j * rows, rows)],
                dst_ref=landed.at[stage, pl.ds(j * rows, rows)],
                send_sem=block_send.at[stage, j],
                recv_sem=block_recv.at[stage, j],
                device_id=(other, j),
                device_id_type=MESH,
            )

        for j in range(n):
            block_copy(j).start()
        @pl.when(begins)
        def _():
            for copy in loads[4:]:
                copy.wait()
            prepare_index()
            prepare_receivers()
            prepare_weights()
            prepare_onehot()
            index_copy.wait()

        for j in range(n):
            arrived(j).wait_recv()

        for b in range(slots // LANES):
            pieces = [[], [], []]
            for j in range(b * LANES // per_device, (b + 1) * LANES // per_device):
                at = j * rows
                pieces[0].append(landed[stage, at : at + per_device, :])
                pieces[1].append(landed[stage, at + per_device : at + 2 * per_device, :])
                ends = landed[stage, at + 2 * per_device : at + rows, :]
                pieces[2].append(jnp.concatenate([ends, pltpu.roll(ends, tail, 1)], axis=0))
            for k in range(3):
                count_k = LANES if k < 2 else tail
                high, low = split(jnp.transpose(jnp.concatenate(pieces[k], axis=0))[:count_k])
                here = slice(k * LANES, k * LANES + count_k)
                mixed_rows = halves
                mixed_rows[here, b * LANES : (b + 1) * LANES] = high
                mixed_rows[here, slots + b * LANES : slots + (b + 1) * LANES] = low
        chunks = elements // CHUNK
        for c in [0, chunks - 1] + list(range(1, chunks - 1)):
            here = slice(c * CHUNK, (c + 1) * CHUNK)
            moved = jnp.dot(halves[:, 0 : 2 * slots], take[:, here], preferred_element_type=F32)
            patched[:, here] = jnp.where(hit[:, here] > 0.5, moved, source[:, here])
            for side in range(2):
                if c == (0 if side == 0 else chunks - 1):

                    @pl.when(me > 0 if side == 0 else me < n - 1)
                    def _():
                        for h in range(2):
                            rim_copy(stage, patched, side, h).start()

        for t in range(elements // LANES):
            here = slice(t * LANES, (t + 1) * LANES)
            at = t * LANES * ROWS
            for k in range(2):
                piece = jnp.transpose(patched[k * LANES : (k + 1) * LANES, here])
                high = piece.astype(BF16).astype(F32)
                table[pl.ds(at + k, LANES, stride=ROWS), :] = high
                table[pl.ds(at + 2 + k, LANES, stride=ROWS), :] = piece - high
            ends = patched[2 * LANES : components, here]
            high = ends.astype(BF16).astype(F32)
            table[pl.ds(at + 4, LANES, stride=ROWS), :] = jnp.transpose(
                jnp.concatenate([high, ends - high], axis=0)
            )
        table[elements * ROWS :, :] = jnp.zeros((8, LANES), F32)

        def to_operand(source_ref, target, f):
            for k in range(ROWS):
                target[f * ROWS + k] = source_ref[pl.ds(k, CHUNK, stride=ROWS), :].astype(BF16)

        def gather(c, target):
            for f in range(FACES):
                where = gathered.at[f]
                for e in range(CHUNK):
                    line = f * (elements // LANES) + c * (CHUNK // LANES) + e // LANES
                    row = index[line, e % LANES]
                    where[e * ROWS : (e + 1) * ROWS, :] = table[pl.ds(row, ROWS), :]
                to_operand(where, target, f)
            size = CHUNK * ROWS
            to_operand(table.at[pl.ds(c * size, size)], target, FACES)

        def contract(c, target):
            parts = []
            for f in range(FACES + 1):
                parts += [target[f * ROWS + k] for k in (0, 1, 2, 3, 0, 1, 4, 4)]
            total[c] = cross(weights[...], jnp.concatenate(parts, axis=1))

        gather(0, even)

        def own(i, carry):
            gather(2 * i + 1, odd)
            contract(2 * i, even)
            gather(lax.rem(2 * i + 2, chunks), even)
            contract(2 * i + 1, odd)
            return carry

        lax.fori_loop(0, chunks // 2, own, 0)

        mean = 0.5 * jnp.asarray(stage, F32)

        for h in range(2):
            for side in range(2):
                inside = me > 0 if side == 0 else me < n - 1
                where = rims.at[stage, h, :, pl.ds(side * half, half)]

                @pl.when(inside)
                def _():
                    rim_copy(stage, patched, 1 - side, h).wait_recv()

                @pl.when(jnp.logical_not(inside))
                def _():
                    where[...] = jnp.zeros((components, half), F32)

            high, low = split(rims[stage, h])
            top = 2 * LANES
            rim_operand[0:top, :] = high[:top]
            rim_operand[top : 2 * top, :] = low[:top]
            rim_operand[2 * top : 3 * top, :] = high[:top]
            at = 3 * top
            for m, value in enumerate((high[top:], low[top:], high[top:], jnp.zeros_like(high[top:]))):
                rim_operand[at + m * tail : at + (m + 1) * tail, :] = value
            for f in range(FACES):
                made = jnp.dot(
                    weights[:, f * width : (f + 1) * width], rim_operand[...], preferred_element_type=F32
                )
                high, low = split(made)
                made_high[:, f * HALO : (f + 1) * HALO] = high
                made_low[:, f * HALO : (f + 1) * HALO] = low

            for c in range(chunks):
                here = slice(c * CHUNK, (c + 1) * CHUNK)
                chosen = onehot[h * FACES * HALO : (h + 1) * FACES * HALO, here]
                sum_c = total[c]
                sum_c = sum_c + jnp.dot(made_high[...], chosen, preferred_element_type=F32)
                sum_c = sum_c + jnp.dot(made_low[...], chosen, preferred_element_type=F32)
                if h == 0:
                    total[c] = sum_c
                else:
                    stepped = patched[:, here] + (STEP * jacobian[:, here]) * sum_c
                    current[:, here] = (1.0 - mean) * stepped + mean * first[:, here]

                    @pl.when(jnp.logical_not(begins))
                    def _():
                        result_copy(c).start()

        for j in range(n):
            block_copy(j).wait_send()
        for side in range(2):

            @pl.when(me > 0 if side == 0 else me < n - 1)
            def _():
                for h in range(2):
                    rim_copy(stage, patched, side, h).wait_send()
        return carry

    lax.fori_loop(0, 2, segment, 0)
    for c in range(elements // CHUNK):
        result_copy(c).wait()


def local(
    n,
    fields,
    jacobian,
    face_links,
    volume_matrix,
    face_matrices,
    patterns,
    donor_index,
    pattern_index,
    receivers,
):
    components, elements = fields.shape[1:]
    slots = donor_index.shape[1]
    rows = slots // n * 5 // 2
    chunks = elements // CHUNK
    width = 8 * LANES
    count = patterns.shape[0]
    result = pl.pallas_call(
        functools.partial(kernel, n),
        out_shape=jax.ShapeDtypeStruct((components, elements), F32),
        in_specs=[pl.BlockSpec(memory_space=pltpu.HBM)] * 9,
        out_specs=pl.BlockSpec(memory_space=pl.ANY),
        scratch_shapes=[
            pltpu.VMEM((1, elements), F32),
            pltpu.VMEM((FACES, 1, elements), jnp.int32),
            pltpu.VMEM((1, slots), jnp.int32),
            pltpu.VMEM((1, slots), jnp.int32),
            pltpu.VMEM((1, slots), jnp.int32),
            pltpu.VMEM(patterns.shape, F32),
            pltpu.VMEM((FACES * elements // LANES, LANES), jnp.int32),
            pltpu.SMEM((FACES * elements // LANES, LANES), jnp.int32),
            pltpu.VMEM((components, elements), F32),
            pltpu.VMEM((components, components), F32),
            pltpu.VMEM((FACES, components, components), F32),
            pltpu.VMEM((2, components, elements), F32),
            pltpu.VMEM((chunks, components, CHUNK), F32),
            pltpu.VMEM((components, 2 * elements), BF16),
            pltpu.VMEM((slots, 2 * elements), BF16),
            pltpu.VMEM((LANES, 3 * count * LANES), BF16),
            pltpu.VMEM((3 * slots, 3 * count * LANES), BF16),
            pltpu.VMEM((slots, 3 * LANES), F32),
            pltpu.VMEM((n * rows, LANES), F32),
            pltpu.VMEM((2, n * rows, LANES), F32),
            pltpu.VMEM((2 * slots, elements), BF16),
            pltpu.VMEM((1, elements), F32),
            pltpu.VMEM((elements * ROWS + 8, LANES), F32),
            pltpu.VMEM((FACES, CHUNK * ROWS, LANES), F32),
            pltpu.VMEM(((FACES + 1) * ROWS, CHUNK, LANES), BF16),
            pltpu.VMEM(((FACES + 1) * ROWS, CHUNK, LANES), BF16),
            pltpu.VMEM((components, (FACES + 1) * width), BF16),
            pltpu.VMEM((2, 2, components, HALO), F32),
            pltpu.VMEM((width, HALO), BF16),
            pltpu.VMEM((components, FACES * HALO), BF16),
            pltpu.VMEM((components, FACES * HALO), BF16),
            pltpu.VMEM((2 * FACES * HALO, elements), BF16),
            pltpu.SemaphoreType.DMA((2, n)),
            pltpu.SemaphoreType.DMA((2, n)),
            pltpu.SemaphoreType.DMA((2, 2, 2)),
            pltpu.SemaphoreType.DMA((2, 2, 2)),
            pltpu.SemaphoreType.DMA((10,)),
            pltpu.SemaphoreType.DMA((chunks,)),
        ],
        compiler_params=pltpu.CompilerParams(
            collective_id=0,
            has_side_effects=True,
            vmem_limit_bytes=62 * 1024 * 1024,
        ),
    )(
        fields[0],
        jacobian,
        jnp.transpose(face_links, (1, 0, 2)),
        donor_index,
        pattern_index,
        receivers,
        patterns,
        volume_matrix[0],
        face_matrices[0],
    )
    return result[None]


def solution(mesh):
    return jax.shard_map(
        functools.partial(local, mesh.shape["elem"]),
        mesh=mesh,
        in_specs=(
            P("sec", None, "elem"),
            P("sec", "elem"),
            P("sec", None, "elem"),
            P("sec", None, None),
            P("sec", None, None, None),
            P(),
            P("sec", "elem"),
            P("sec", "elem"),
            P("sec", "elem"),
        ),
        out_specs=P("sec", None, "elem"),
        check_vma=False,
    )
```

```python
import functools

import jax
import jax.numpy as jnp
from jax import lax
from jax.experimental import pallas as pl
from jax.experimental.pallas import tpu as pltpu
from jax.sharding import PartitionSpec as P

HALO = 256
LANES = 128
CHUNK = 256
ROWS = 5
FACES = 6
STEP = 0.25
MESH = pl.DeviceIdType.MESH
F32 = jnp.float32
BF16 = jnp.bfloat16


def split(value):
    high = value.astype(BF16)
    return high, (value - high.astype(F32)).astype(BF16)


def cross(a, b):
    return lax.dot_general(a, b, (((1,), (1,)), ((), ())), preferred_element_type=F32)


def iota(shape, dim):
    return lax.broadcasted_iota(jnp.int32, shape, dim)


def column(row):
    return jnp.transpose(jnp.broadcast_to(row.astype(F32), (LANES, LANES))).astype(jnp.int32)


def kernel(
    n,
    fields_hbm,
    jacobian_hbm,
    links_hbm,
    donors_hbm,
    choose_hbm,
    receivers_hbm,
    patterns_hbm,
    volume_hbm,
    faces_hbm,
    out_hbm,
    jacobian,
    links,
    donors,
    choose,
    receivers,
    patterns,
    reach,
    index,
    current,
    volume,
    faces,
    states,
    total,
    halves,
    give,
    twice,
    mixed,
    donated,
    outgoing,
    landed,
    take,
    hit,
    table,
    gathered,
    even,
    odd,
    weights,
    rims,
    rim_operand,
    partial,
    made_high,
    made_low,
    onehot,
    block_send,
    block_recv,
    rim_send,
    rim_recv,
    load,
    store,
):
    sec, me = lax.axis_index("sec"), lax.axis_index("elem")
    other = 1 - sec
    components, elements = current.shape
    slots = donors.shape[1]
    per_device = slots // n
    rows = 2 * per_device + per_device // 2
    tail = components - 2 * LANES
    width = 8 * LANES
    half = HALO // 2

    barrier = pltpu.get_barrier_semaphore()
    for j in range(n):
        pl.semaphore_signal(barrier, inc=1, device_id=(other, j), device_id_type=MESH)

    @pl.when(me > 0)
    def _():
        pl.semaphore_signal(barrier, inc=1, device_id=(sec, me - 1), device_id_type=MESH)

    @pl.when(me < n - 1)
    def _():
        pl.semaphore_signal(barrier, inc=1, device_id=(sec, me + 1), device_id_type=MESH)

    pairs = (
        (donors_hbm, donors),
        (choose_hbm, choose),
        (patterns_hbm, patterns),
        (fields_hbm, current),
        (receivers_hbm, receivers),
        (links_hbm, links),
        (jacobian_hbm, jacobian),
        (volume_hbm, volume),
        (faces_hbm, faces),
    )
    loads = [pltpu.make_async_copy(src, dst, load.at[i]) for i, (src, dst) in enumerate(pairs)]
    for copy in loads[:4]:
        copy.start()
    index_copy = pltpu.make_async_copy(reach, index, load.at[len(loads)])

    for copy in loads[:3]:
        copy.wait()

    for b in range(slots // LANES):
        rows_b = slice(b * LANES, (b + 1) * LANES)
        donor = column(donors[:, rows_b])
        for t in range(elements // LANES):
            lane = iota((LANES, LANES), 1) + t * LANES
            one = jnp.where(donor == lane, 1.0, 0.0).astype(BF16)
            give[rows_b, t * LANES : (t + 1) * LANES] = one
            give[rows_b, elements + t * LANES : elements + (t + 1) * LANES] = one
    kinds = [column(choose[:, b * LANES : (b + 1) * LANES]) for b in range(slots // LANES)]
    count = patterns.shape[0]
    for p in range(count):
        one = patterns[p]
        none = jnp.zeros_like(one)
        both = jnp.concatenate(
            [jnp.concatenate([one, none], axis=1), jnp.concatenate([none, one], axis=1)], axis=0
        )
        high, low = split(both)
        for part, value in enumerate((high, high, low)):
            at = (part * count + p) * LANES
            twice[:, at : at + LANES] = value

    def prepare_index():
        for f in range(FACES):
            inner = links[f] - HALO
            owned = (inner >= 0) & (inner < elements)
            row = jnp.where(owned, inner, elements) * ROWS
            for t in range(elements // LANES):
                at = f * (elements // LANES) + t
                reach[at : at + 1, :] = row[:, t * LANES : (t + 1) * LANES]
        index_copy.start()

    def prepare_receivers():
        for t in range(elements // LANES):
            lane = iota((LANES, LANES), 1) + t * LANES
            here = slice(t * LANES, (t + 1) * LANES)
            seen = jnp.zeros((1, LANES), F32)
            for b in range(slots // LANES):
                one = jnp.where(column(receivers[:, b * LANES : (b + 1) * LANES]) == lane, 1.0, 0.0)
                seen = seen + jnp.sum(one, axis=0, keepdims=True)
                take[b * LANES : (b + 1) * LANES, here] = one.astype(BF16)
                take[slots + b * LANES : slots + (b + 1) * LANES, here] = one.astype(BF16)
            hit[:, here] = seen

    def prepare_weights():
        for f in range(FACES + 1):
            matrix = volume if f == FACES else faces.at[f]
            high, low = split(matrix[:, 0 : 2 * LANES])
            ends = matrix[:, 2 * LANES : components]
            end_high, end_low = split(jnp.concatenate([ends, ends], axis=1))
            lane = iota(end_low.shape, 1)
            end_low = jnp.where(lane < tail, end_low.astype(F32), 0.0).astype(BF16)
            at = f * width
            weights[:, at : at + 2 * LANES] = high
            weights[:, at + 2 * LANES : at + 4 * LANES] = high
            weights[:, at + 4 * LANES : at + 6 * LANES] = low
            weights[:, at + 6 * LANES : at + 7 * LANES] = end_high
            weights[:, at + 7 * LANES : at + 8 * LANES] = end_low

    def prepare_onehot():
        def body(f, carry):
            for h in range(2):
                for side in range(2):
                    begin = side * (HALO + elements) + h * half
                    for t in range(elements // CHUNK):
                        here = slice(t * CHUNK, (t + 1) * CHUNK)
                        row = links[f, :, here]
                        one = jnp.where(row == iota((half, CHUNK), 0) + begin, 1.0, 0.0)
                        at = pl.multiple_of((h * FACES + f) * HALO + side * half, half)
                        onehot[pl.ds(at, half), here] = one.astype(BF16)
            return carry

        lax.fori_loop(0, FACES, body, 0)

    top = 2 * LANES
    groups = ((0, 0, components), (1, 0, top), (1, top, components))

    def rim_copy(stage, source, side, g):
        target = me - 1 if side == 0 else me + 1
        h, low, high = groups[g]
        begin = h * half if side == 0 else elements - HALO + h * half
        return pltpu.make_async_remote_copy(
            src_ref=source.at[pl.ds(low, high - low), pl.ds(begin, half)],
            dst_ref=rims.at[stage, h, pl.ds(low, high - low), pl.ds((1 - side) * half, half)],
            send_sem=rim_send.at[stage, side, g],
            recv_sem=rim_recv.at[stage, 1 - side, g],
            device_id=(sec, target),
            device_id_type=MESH,
        )

    def result_copy(c):
        here = pl.ds(c * CHUNK, CHUNK)
        return pltpu.make_async_copy(current.at[:, here], out_hbm.at[:, here], store.at[c])

    loads[3].wait()
    for copy in loads[4:]:
        copy.start()
    first = states.at[0]

    def segment(stage, carry):
        source = current
        patched = states.at[stage]
        begins = stage == 0

        high, low = split(source[...])
        halves[:, 0:elements] = high
        halves[:, elements:] = low
        donated[:, 0:components] = cross(give[...], halves[...])
        for b in range(slots // LANES):
            for k in range(3):
                piece = donated[b * LANES : (b + 1) * LANES, k * LANES : (k + 1) * LANES]
                if k == 2:
                    piece = jnp.where(iota(piece.shape, 1) < tail, piece, 0.0)
                high = piece.astype(BF16).astype(F32)
                for p in range(count):
                    mask = kinds[b] == p
                    big = jnp.where(mask, high, 0.0).astype(BF16)
                    small = jnp.where(mask, piece - high, 0.0).astype(BF16)
                    row = k * slots + b * LANES
                    for part, value in enumerate((big, small, big)):
                        at = (part * count + p) * LANES
                        mixed[row : row + LANES, at : at + LANES] = value
        result = cross(mixed[...], twice[...])
        quarter = per_device // 2
        for j in range(n):
            at, slot = j * rows, j * per_device
            outgoing[at : at + per_device, :] = result[slot : slot + per_device]
            outgoing[at + per_device : at + 2 * per_device, :] = result[slots + slot : slots + slot + per_device]
            ends = result[2 * slots + slot : 2 * slots + slot + per_device]
            outgoing[at + 2 * per_device : at + rows, :] = ends[:quarter] + pltpu.roll(ends, tail, 1)[quarter:]

        @pl.when(begins)
        def _():
            heard = n + (me > 0).astype(jnp.int32) + (me < n - 1).astype(jnp.int32)
            pl.semaphore_wait(barrier, heard)

        def block_copy(j):
            return pltpu.make_async_remote_copy(
                src_ref=outgoing.at[pl.ds(j * rows, rows)],
                dst_ref=landed.at[stage, pl.ds(me * rows, rows)],
                send_sem=block_send.at[stage, j],
                recv_sem=block_recv.at[stage, me],
                device_id=(other, j),
                device_id_type=MESH,
            )

        def arrived(j):
            return pltpu.make_async_remote_copy(
                src_ref=outgoing.at[pl.ds(j * rows, rows)],
                dst_ref=landed.at[stage, pl.ds(j * rows, rows)],
                send_sem=block_send.at[stage, j],
                recv_sem=block_recv.at[stage, j],
                device_id=(other, j),
                device_id_type=MESH,
            )

        for j in range(n):
            block_copy(j).start()
        @pl.when(begins)
        def _():
            for copy in loads[4:]:
                copy.wait()
            prepare_index()
            prepare_receivers()
            prepare_weights()
            prepare_onehot()
            index_copy.wait()

        for j in range(n):
            arrived(j).wait_recv()

        for b in range(slots // LANES):
            pieces = [[], [], []]
            for j in range(b * LANES // per_device, (b + 1) * LANES // per_device):
                at = j * rows
                pieces[0].append(landed[stage, at : at + per_device, :])
                pieces[1].append(landed[stage, at + per_device : at + 2 * per_device, :])
                ends = landed[stage, at + 2 * per_device : at + rows, :]
                pieces[2].append(jnp.concatenate([ends, pltpu.roll(ends, tail, 1)], axis=0))
            for k in range(3):
                count_k = LANES if k < 2 else tail
                high, low = split(jnp.transpose(jnp.concatenate(pieces[k], axis=0))[:count_k])
                here = slice(k * LANES, k * LANES + count_k)
                mixed_rows = halves
                mixed_rows[here, b * LANES : (b + 1) * LANES] = high
                mixed_rows[here, slots + b * LANES : slots + (b + 1) * LANES] = low
        chunks = elements // CHUNK
        for c in [0, chunks - 1] + list(range(1, chunks - 1)):
            here = slice(c * CHUNK, (c + 1) * CHUNK)
            moved = jnp.dot(halves[:, 0 : 2 * slots], take[:, here], preferred_element_type=F32)
            patched[:, here] = jnp.where(hit[:, here] > 0.5, moved, source[:, here])
            for side in range(2):
                if c == (0 if side == 0 else chunks - 1):

                    @pl.when(me > 0 if side == 0 else me < n - 1)
                    def _():
                        for g in range(len(groups)):
                            rim_copy(stage, patched, side, g).start()

        for t in range(elements // LANES):
            here = slice(t * LANES, (t + 1) * LANES)
            at = t * LANES * ROWS
            for k in range(2):
                piece = jnp.transpose(patched[k * LANES : (k + 1) * LANES, here])
                high = piece.astype(BF16).astype(F32)
                table[pl.ds(at + k, LANES, stride=ROWS), :] = high
                table[pl.ds(at + 2 + k, LANES, stride=ROWS), :] = piece - high
            ends = patched[2 * LANES : components, here]
            high = ends.astype(BF16).astype(F32)
            table[pl.ds(at + 4, LANES, stride=ROWS), :] = jnp.transpose(
                jnp.concatenate([high, ends - high], axis=0)
            )
        table[elements * ROWS :, :] = jnp.zeros((8, LANES), F32)

        def to_operand(source_ref, target, f):
            for k in range(ROWS):
                target[f * ROWS + k] = source_ref[pl.ds(k, CHUNK, stride=ROWS), :].astype(BF16)

        def gather(c, target):
            for f in range(FACES):
                where = gathered.at[f]
                for e in range(CHUNK):
                    line = f * (elements // LANES) + c * (CHUNK // LANES) + e // LANES
                    row = index[line, e % LANES]
                    where[e * ROWS : (e + 1) * ROWS, :] = table[pl.ds(row, ROWS), :]
                to_operand(where, target, f)
            size = CHUNK * ROWS
            to_operand(table.at[pl.ds(c * size, size)], target, FACES)

        def contract(c, target):
            parts = []
            for f in range(FACES + 1):
                parts += [target[f * ROWS + k] for k in (0, 1, 2, 3, 0, 1, 4, 4)]
            total[c] = cross(weights[...], jnp.concatenate(parts, axis=1))

        buffers = (even, odd)
        gather(0, even)
        for c in range(chunks):
            if c + 1 < chunks:
                gather(c + 1, buffers[(c + 1) % 2])
            contract(c, buffers[c % 2])

        mean = 0.5 * jnp.asarray(stage, F32)

        deep = 3 * top
        for g, (h, low_row, high_row) in enumerate(groups):
            rows_g = pl.ds(low_row, high_row - low_row)
            for side in range(2):
                inside = me > 0 if side == 0 else me < n - 1
                where = rims.at[stage, h, rows_g, pl.ds(side * half, half)]

                @pl.when(inside)
                def _():
                    rim_copy(stage, patched, 1 - side, g).wait_recv()

                @pl.when(jnp.logical_not(inside))
                def _():
                    where[...] = jnp.zeros(where.shape, F32)

            if low_row == 0:
                high, low = split(rims[stage, h, 0:top])
                rim_operand[0:top, :] = high
                rim_operand[top : 2 * top, :] = low
                rim_operand[2 * top : deep, :] = high
            if high_row == components:
                high, low = split(rims[stage, h, top:components])
                for m, value in enumerate((high, low, high, jnp.zeros_like(high))):
                    rim_operand[deep + m * tail : deep + (m + 1) * tail, :] = value
            begin, end = 0 if low_row == 0 else deep, deep if high_row == top else width
            for f in range(FACES):
                here = slice(f * HALO, (f + 1) * HALO)
                made = jnp.dot(
                    weights[:, f * width + begin : f * width + end],
                    rim_operand[begin:end, :],
                    preferred_element_type=F32,
                )
                if high_row == top:
                    partial[:, here] = made
                    continue
                if low_row == top:
                    made = made + partial[:, here]
                high, low = split(made)
                made_high[:, here] = high
                made_low[:, here] = low
            if high_row == top:
                continue

            for c in range(chunks):
                here = slice(c * CHUNK, (c + 1) * CHUNK)
                chosen = onehot[h * FACES * HALO : (h + 1) * FACES * HALO, here]
                sum_c = total[c]
                sum_c = sum_c + jnp.dot(made_high[...], chosen, preferred_element_type=F32)
                sum_c = sum_c + jnp.dot(made_low[...], chosen, preferred_element_type=F32)
                if h == 0:
                    total[c] = sum_c
                else:
                    stepped = patched[:, here] + (STEP * jacobian[:, here]) * sum_c
                    current[:, here] = (1.0 - mean) * stepped + mean * first[:, here]

                    @pl.when(jnp.logical_not(begins))
                    def _():
                        result_copy(c).start()

        for j in range(n):
            block_copy(j).wait_send()
        for side in range(2):

            @pl.when(me > 0 if side == 0 else me < n - 1)
            def _():
                for g in range(len(groups)):
                    rim_copy(stage, patched, side, g).wait_send()
        return carry

    lax.fori_loop(0, 2, segment, 0)
    for c in range(elements // CHUNK):
        result_copy(c).wait()


def local(
    n,
    fields,
    jacobian,
    face_links,
    volume_matrix,
    face_matrices,
    patterns,
    donor_index,
    pattern_index,
    receivers,
):
    components, elements = fields.shape[1:]
    slots = donor_index.shape[1]
    rows = slots // n * 5 // 2
    chunks = elements // CHUNK
    width = 8 * LANES
    count = patterns.shape[0]
    result = pl.pallas_call(
        functools.partial(kernel, n),
        out_shape=jax.ShapeDtypeStruct((components, elements), F32),
        in_specs=[pl.BlockSpec(memory_space=pltpu.HBM)] * 9,
        out_specs=pl.BlockSpec(memory_space=pl.ANY),
        scratch_shapes=[
            pltpu.VMEM((1, elements), F32),
            pltpu.VMEM((FACES, 1, elements), jnp.int32),
            pltpu.VMEM((1, slots), jnp.int32),
            pltpu.VMEM((1, slots), jnp.int32),
            pltpu.VMEM((1, slots), jnp.int32),
            pltpu.VMEM(patterns.shape, F32),
            pltpu.VMEM((FACES * elements // LANES, LANES), jnp.int32),
            pltpu.SMEM((FACES * elements // LANES, LANES), jnp.int32),
            pltpu.VMEM((components, elements), F32),
            pltpu.VMEM((components, components), F32),
            pltpu.VMEM((FACES, components, components), F32),
            pltpu.VMEM((2, components, elements), F32),
            pltpu.VMEM((chunks, components, CHUNK), F32),
            pltpu.VMEM((components, 2 * elements), BF16),
            pltpu.VMEM((slots, 2 * elements), BF16),
            pltpu.VMEM((LANES, 3 * count * LANES), BF16),
            pltpu.VMEM((3 * slots, 3 * count * LANES), BF16),
            pltpu.VMEM((slots, 3 * LANES), F32),
            pltpu.VMEM((n * rows, LANES), F32),
            pltpu.VMEM((2, n * rows, LANES), F32),
            pltpu.VMEM((2 * slots, elements), BF16),
            pltpu.VMEM((1, elements), F32),
            pltpu.VMEM((elements * ROWS + 8, LANES), F32),
            pltpu.VMEM((FACES, CHUNK * ROWS, LANES), F32),
            pltpu.VMEM(((FACES + 1) * ROWS, CHUNK, LANES), BF16),
            pltpu.VMEM(((FACES + 1) * ROWS, CHUNK, LANES), BF16),
            pltpu.VMEM((components, (FACES + 1) * width), BF16),
            pltpu.VMEM((2, 2, components, HALO), F32),
            pltpu.VMEM((width, HALO), BF16),
            pltpu.VMEM((components, FACES * HALO), F32),
            pltpu.VMEM((components, FACES * HALO), BF16),
            pltpu.VMEM((components, FACES * HALO), BF16),
            pltpu.VMEM((2 * FACES * HALO, elements), BF16),
            pltpu.SemaphoreType.DMA((2, n)),
            pltpu.SemaphoreType.DMA((2, n)),
            pltpu.SemaphoreType.DMA((2, 2, 3)),
            pltpu.SemaphoreType.DMA((2, 2, 3)),
            pltpu.SemaphoreType.DMA((10,)),
            pltpu.SemaphoreType.DMA((chunks,)),
        ],
        compiler_params=pltpu.CompilerParams(
            collective_id=0,
            has_side_effects=True,
            vmem_limit_bytes=62 * 1024 * 1024,
        ),
    )(
        fields[0],
        jacobian,
        jnp.transpose(face_links, (1, 0, 2)),
        donor_index,
        pattern_index,
        receivers,
        patterns,
        volume_matrix[0],
        face_matrices[0],
    )
    return result[None]


def solution(mesh):
    return jax.shard_map(
        functools.partial(local, mesh.shape["elem"]),
        mesh=mesh,
        in_specs=(
            P("sec", None, "elem"),
            P("sec", "elem"),
            P("sec", None, "elem"),
            P("sec", None, None),
            P("sec", None, None, None),
            P(),
            P("sec", "elem"),
            P("sec", "elem"),
            P("sec", "elem"),
        ),
        out_specs=P("sec", None, "elem"),
        check_vma=False,
    )
```
